32 devices in a mesh: rows: 4 (over y, x), cols: 8 (over z, core).
Axes of the slice: x: 2, y: 2, z: 4, core: 2. Of those that a mesh axis runs over, the one named last changes fastest.
Arguments:
- anomalies: float32 [16384, 1024], P('rows', 'cols'), may hold values from -75 to 75
- pairing: int32 [2, 8], replicated, may hold values from 0 to 7, as said below
Outputs:
- rotated: float32 [16384, 1024], P('rows', 'cols')
The draws below stay inside these ranges and needn't reach their ends.
Inputs may be any that keep to these rules, and one draw needn't show every extreme that they name: pairing[r, b] = b XOR m_r with one m_r for the whole row r; m_0 is neither 0 nor 1024 // 128 - 1, and for odd r m_r is m_0 with every bit of 7 flipped, for even r it is m_0.
All inputs are finite; a program needn't handle non-finite values.
Results may differ from the reference program's by a relative error of at most 0.0003.
Values sent between devices are 32-bit elements; how exact they have to be, the bound alone decides.
A program may use at most 128 MiB of HBM per device.

```python
import math
import jax
import jax.numpy as jnp
from jax import lax

BLK = 128
SHIFTS = 8
ROUNDS = 2
SOUNDINGS = 16384
MEMBERS = 1024


def draw_anomalies(key, part):
    subkeys = jax.random.split(key, 5)
    position = (jnp.arange(SOUNDINGS, dtype=jnp.float32)[:, None] + 0.5) / SOUNDINGS
    rising = 1.0 + 2.0 * position
    roughness = jax.random.uniform(subkeys[0], (SOUNDINGS, 1), jnp.float32, 0.5, 1.5)
    column_scale = jnp.exp(jax.random.uniform(subkeys[1], (1, MEMBERS), jnp.float32, math.log(0.3), math.log(3.0)))
    row_factor = jnp.clip(jax.random.normal(subkeys[2], (SOUNDINGS, 1), jnp.float32), -5.0, 5.0)
    column_factor = jnp.clip(jax.random.normal(subkeys[3], (1, MEMBERS), jnp.float32), -5.0, 5.0)
    noise_field = jnp.clip(jax.random.normal(subkeys[4], (SOUNDINGS, MEMBERS), jnp.float32), -5.0, 5.0)
    strength = 0.2 + 0.8 * position
    values = 0.3 * rising * roughness * (noise_field * column_scale + strength * row_factor * column_factor)
    return values.astype(jnp.float32)


def draw_pairing(key, part):
    block_total = MEMBERS // BLK
    first_mask = jax.random.randint(key, (), 1, block_total - 1)
    all_bits = block_total - 1
    round_ids = jnp.arange(ROUNDS)
    round_masks = jnp.where(round_ids % 2 == 0, first_mask, jnp.bitwise_xor(first_mask, all_bits))
    indices = jnp.arange(block_total)
    return jnp.bitwise_xor(indices[None, :], round_masks[:, None]).astype(jnp.int32)


def setup_inputs(seed: int = 0) -> dict:
    arg_keys = jax.random.split(jax.random.key(seed), 3)
    return {
        "anomalies": draw_anomalies(jax.random.fold_in(arg_keys[2], 71), 0),
        "pairing": draw_pairing(jax.random.fold_in(arg_keys[2], 71), 0),
    }


TIE_GUARD = 1e-06

def block_product(left, right):
    return jnp.dot(left.T, right, precision=lax.Precision.HIGHEST, preferred_element_type=jnp.float32)

def apply_turn(data, coef):
    return jnp.dot(data, coef, precision=lax.Precision.HIGHEST, preferred_element_type=jnp.float32)

def rotate_pair(gram_ll, gram_lr, gram_rl, gram_rr, shifts):
    width = gram_ll.shape[0]
    eye_block = jnp.eye(width, dtype=jnp.float32)
    empty_block = jnp.zeros((width, width), jnp.float32)
    turn_ll, turn_lr, turn_rl, turn_rr = (eye_block, empty_block, empty_block, eye_block)
    for shift_step in range(shifts):
        if shift_step > 0:
            gram_lr = jnp.roll(gram_lr, -1, axis=1)
            gram_rl = jnp.roll(gram_rl, -1, axis=0)
            gram_rr = jnp.roll(jnp.roll(gram_rr, -1, axis=0), -1, axis=1)
            turn_lr = jnp.roll(turn_lr, -1, axis=1)
            turn_rr = jnp.roll(turn_rr, -1, axis=1)
        left_diag = jnp.diagonal(gram_ll)
        right_diag = jnp.diagonal(gram_rr)
        cross_diag = jnp.diagonal(gram_lr)
        gap_value = right_diag - left_diag
        gap_sign = jnp.where(gap_value >= 0.0, 1.0, -1.0).astype(gap_value.dtype)
        denom = jnp.abs(gap_value) + jnp.sqrt(gap_value * gap_value + 4.0 * cross_diag * cross_diag) + TIE_GUARD * (left_diag + right_diag)
        tangent = 2.0 * cross_diag * gap_sign / denom
        cosine = 1.0 / jnp.sqrt(1.0 + tangent * tangent)
        sine_value = cosine * tangent
        col_cos = cosine[None, :]
        col_sin = sine_value[None, :]
        upper_left = gram_ll * col_cos - gram_lr * col_sin
        upper_right = gram_ll * col_sin + gram_lr * col_cos
        lower_left = gram_rl * col_cos - gram_rr * col_sin
        lower_right = gram_rl * col_sin + gram_rr * col_cos
        row_cos = cosine[:, None]
        row_sin = sine_value[:, None]
        gram_ll = row_cos * upper_left - row_sin * lower_left
        gram_lr = row_cos * upper_right - row_sin * lower_right
        gram_rl = row_sin * upper_left + row_cos * lower_left
        gram_rr = row_sin * upper_right + row_cos * lower_right
        new_ll = turn_ll * col_cos - turn_lr * col_sin
        new_lr = turn_ll * col_sin + turn_lr * col_cos
        new_rl = turn_rl * col_cos - turn_rr * col_sin
        new_rr = turn_rl * col_sin + turn_rr * col_cos
        turn_ll, turn_lr, turn_rl, turn_rr = (new_ll, new_lr, new_rl, new_rr)
    back_steps = shifts - 1
    turn_lr = jnp.roll(turn_lr, back_steps, axis=1)
    turn_rr = jnp.roll(turn_rr, back_steps, axis=1)
    gram_rr = jnp.roll(jnp.roll(gram_rr, back_steps, axis=0), back_steps, axis=1)
    return ((turn_ll, turn_lr, turn_rl, turn_rr), (gram_ll, gram_rr))

def pair_output(current, pair_row, block_index):
    partner = pair_row[block_index].astype(jnp.int32)
    low_index = jnp.minimum(block_index, partner).astype(jnp.int32)
    high_index = jnp.maximum(block_index, partner).astype(jnp.int32)
    low_cols = lax.dynamic_slice_in_dim(current, (low_index * BLK).astype(jnp.int32), BLK, 1)
    high_cols = lax.dynamic_slice_in_dim(current, (high_index * BLK).astype(jnp.int32), BLK, 1)
    gram_ll = block_product(low_cols, low_cols)
    gram_lr = block_product(low_cols, high_cols)
    gram_rr = block_product(high_cols, high_cols)
    turns, grams = rotate_pair(gram_ll, gram_lr, gram_lr.T, gram_rr, SHIFTS)
    is_low = block_index == low_index
    coef_low = jnp.where(is_low, turns[0], turns[1])
    coef_high = jnp.where(is_low, turns[2], turns[3])
    return apply_turn(low_cols, coef_low) + apply_turn(high_cols, coef_high)

def reference(anomalies, pairing):
    block_total = MEMBERS // BLK
    current = anomalies
    for round_index in range(ROUNDS):
        pair_row = pairing[round_index]

        def one_block(block_index, current=current, pair_row=pair_row):
            return pair_output(current, pair_row, block_index)
        stacked = lax.map(one_block, jnp.arange(block_total, dtype=jnp.int32))
        current = jnp.transpose(stacked, (1, 0, 2)).reshape(SOUNDINGS, MEMBERS)
    return current
```

```python
from functools import partial

import jax
import jax.numpy as jnp
from jax import lax
from jax.experimental import pallas as pl
from jax.experimental.pallas import tpu as pltpu
from jax.sharding import PartitionSpec as P

SHIFTS = 8
TIE_GUARD = 1e-06
BAND = 2 * SHIFTS
PAIRS = 10
MESH = pl.DeviceIdType.MESH
HIGHEST = lax.Precision.HIGHEST
UNITS = 8
PARTS = (3, 3, 1, 1)
EXTRAS = (2, 1, 3)


def dot(left, right):
    return jnp.dot(left, right, precision=HIGHEST, preferred_element_type=jnp.float32)


def dot_t(left, right):
    return lax.dot_general(
        left,
        right,
        (((0,), (0,)), ((), ())),
        precision=HIGHEST,
        preferred_element_type=jnp.float32,
    )


def halves(value):
    high = value.astype(jnp.bfloat16)
    return high, (value - high.astype(jnp.float32)).astype(jnp.bfloat16)


def dot_3(left, right):
    a, b = halves(left)
    c, d = halves(right)
    product = partial(jnp.dot, preferred_element_type=jnp.float32)
    return product(a, c) + (product(a, d) + product(b, c))


def quad_blocks(pairing, count, g):
    m0 = pairing[0, 0]
    m1 = pairing[1, 0]
    lower_mask = jnp.minimum(m0, m1)
    low_bits = jnp.int32(0)
    for bit in range(1, count.bit_length() - 1):
        low_bits = jnp.where(lower_mask >= (1 << bit), (1 << bit) - 1, low_bits)
    rest = g & low_bits
    q0 = rest + 2 * (g - rest)
    return q0, q0 ^ m0, q0 ^ m1, q0 ^ (count - 1)


def lane_bit(shape, bit):
    return (lax.broadcasted_iota(jnp.int32, shape, 1) & (1 << bit)) != 0


def to_bands(block):
    w = block.shape[0]
    for bit in range(w.bit_length() - 1):
        block = jnp.where(
            lane_bit(block.shape, bit), pltpu.roll(block, w - (1 << bit), 0), block
        )
    return jnp.concatenate([block[w - BAND :], block[:BAND]], axis=0)


def from_bands(bands):
    w = bands.shape[1]
    block = jnp.concatenate(
        [bands[BAND:], jnp.zeros((w - 2 * BAND, w), jnp.float32), bands[:BAND]], axis=0
    )
    for bit in range(w.bit_length() - 1):
        block = jnp.where(lane_bit(block.shape, bit), pltpu.roll(block, 1 << bit, 0), block)
    return block


def turn_pairs(gram, turn, pairs):
    _, depth, sides, w = gram.shape

    def lane(value):
        return pltpu.roll(value.reshape(depth * sides, w), w - 1, 1).reshape(depth, sides, w)

    def later(value):
        return jnp.concatenate([value[-1:], value[:-1]], axis=0)

    def sooner(value):
        return jnp.concatenate([value[1:], value[:1]], axis=0)

    def swap(value):
        return jnp.concatenate([value[:, pairs:], value[:, :pairs]], axis=1)

    def ahead(value):
        return jnp.stack([pltpu.roll(value, (BAND - r) % w, 1) if r != BAND else value for r in range(depth)])

    lower = lax.broadcasted_iota(jnp.int32, (depth, sides, w), 1) >= pairs

    @pl.loop(0, SHIFTS)
    def _(step):
        g_l, g_r = gram[0], gram[1]
        a, e, g = gram[0, BAND, :pairs], gram[1, BAND, pairs:], gram[1, BAND, :pairs]
        gap = e - a
        sign = jnp.where(gap >= 0.0, 1.0, -1.0)
        denom = jnp.abs(gap) + jnp.sqrt(gap * gap + 4.0 * g * g) + TIE_GUARD * (a + e)
        tangent = 2.0 * g * sign / denom
        cosine = 1.0 / jnp.sqrt(1.0 + tangent * tangent)
        sine = cosine * tangent
        c_2 = jnp.concatenate([cosine, cosine], axis=0)
        s_2 = jnp.concatenate([sine, sine], axis=0)
        c_d = ahead(c_2)
        s_d = ahead(jnp.concatenate([-sine, sine], axis=0))
        t_l = g_l * c_2 - g_r * s_2
        t_r = g_l * s_2 + g_r * c_2
        t_l = c_d * t_l + s_d * swap(t_l)
        t_r = lane(c_d * t_r + s_d * swap(t_r))
        gram[0] = jnp.where(lower, sooner(t_l), t_l)
        gram[1] = jnp.where(lower, t_r, later(t_r))
        v_l, v_r = turn[0], turn[1]
        turn[0] = v_l * c_2 - v_r * s_2
        turn[1] = later(lane(v_l * s_2 + v_r * c_2))


def spans(sizes, unit):
    out, at = [], 0
    for size in sizes:
        out.append((at * unit, (at + size) * unit))
        at += size
    return out


def fused_kernel(count, split, unit, names, pairing, x_ref, out_ref, *refs):
    ref = dict(zip(names, refs))
    near = [ref["near%d" % i] for i in range(len(PARTS))]
    far = [ref["far%d" % i] for i in range(len(EXTRAS))]
    near_at, far_at = spans(PARTS, unit), spans(EXTRAS, unit)
    slab, kept = UNITS * unit, sum(EXTRAS) * unit
    half, groups = count // 2, count // 4
    w = x_ref.shape[2]
    lo, hi = slice(0, w), slice(w, 2 * w)
    me, r = lax.axis_index("cols"), lax.axis_index("rows")
    side, pos = me // half, me % half
    across = [(1 - side) * half + (pos + j) % half for j in range(half)]
    beside = [side * half + (pos + j) % half for j in range(1, half)]
    others = across + beside
    masks = (pairing[0, 0], pairing[1, 0], count - 1)
    sent = []

    barrier = pltpu.get_barrier_semaphore()
    for dest in others:
        pl.semaphore_signal(barrier, inc=1, device_id={"cols": dest}, device_id_type=MESH)
    for d in range(1, split):
        pl.semaphore_signal(
            barrier, inc=1, device_id={"rows": (r + d) % split}, device_id_type=MESH
        )
    pl.semaphore_wait(barrier, count + split - 2)

    def remote(src, dst, send, recv, axis, peer):
        return pltpu.make_async_remote_copy(
            src_ref=src,
            dst_ref=dst,
            send_sem=send,
            recv_sem=recv,
            device_id={axis: peer},
            device_id_type=MESH,
        )

    def send(*args):
        copy = remote(*args)
        copy.start()
        sent.append(copy)

    def give(number, land, at, owner):
        rows = pl.ds(at[0], at[1] - at[0])
        for i, dest in enumerate(others):
            src = x_ref.at[owner(dest), rows]
            send(src, land.at[me], ref["give"].at[number, i], ref["get"].at[number, me], "cols", dest)

    def keep(number, land, at, owner):
        rows = pl.ds(at[0], at[1] - at[0])
        return pltpu.make_async_copy(x_ref.at[owner, rows], land.at[me], ref["own"].at[number])

    def take(number, land):
        for source in others:
            remote(
                land.at[source], land.at[source], ref["give"].at[number, 0], ref["get"].at[number, source], "cols", source
            ).wait_recv()

    def mirror(d):
        return count - 1 - d

    kept_copies = []
    for i, at in enumerate(near_at):
        give(i, near[i], at, lambda d: d)
        kept_copies.append(keep(i, near[i], at, me))
        kept_copies[-1].start()

    def give_far(i):
        n = len(PARTS) + i
        give(n, far[i], far_at[i], mirror)
        copy = keep(n, far[i], far_at[i], mirror(me))
        copy.start()
        kept_copies.append(copy)

    give_far(0)

    acc, bands = ref["acc"], ref["bands"]
    for i, land in enumerate(near):
        kept_copies[i].wait()
        take(i, land)
        for g in range(groups):
            x = [land[q] for q in quad_blocks(pairing, count, g)]
            a = jnp.concatenate(x[:2], axis=1)
            b = jnp.concatenate(x[2:], axis=1)
            for k, block in enumerate((dot_t(a, a), dot_t(b, b), dot_t(b, a))):
                acc[g, k] = block if i == 0 else acc[g, k] + block
    for g in range(groups):
        places = [(0, lo, lo), (0, hi, lo), (0, hi, hi), (1, lo, lo), (1, hi, lo), (1, hi, hi)]
        places += [(2, lo, lo), (2, lo, hi), (2, hi, lo), (2, hi, hi)]
        for i, (k, rows, cols) in enumerate(places):
            at = g * PAIRS + i
            bands[at // bands.shape[1], at % bands.shape[1]] = to_bands(acc[g, k, rows, cols])

    landed, part, slots, whole, summed = (
        ref[n] for n in ("landed", "part", "slots", "whole", "summed")
    )

    def stage(number, axis, me, n, source, dest):
        copies = []
        for d in range(1, n):
            peer = (me + d) % n
            copy = remote(
                source(peer), dest(d), ref["sum_s"].at[number, d], ref["sum_r"].at[number, d], axis, peer
            )
            copy.start()
            copies.append(copy)
        sent.extend(copies)
        return copies

    def arrive(copies):
        for copy in copies:
            copy.wait_recv()

    arrive(stage(0, "rows", r, split, lambda p: bands.at[p], lambda d: landed.at[d]))
    total = bands[r]
    for d in range(1, split):
        total = total + landed[d]
    part[...] = total.reshape(part.shape)
    copies = stage(1, "cols", me, count, lambda p: part.at[p], lambda d: slots.at[d])
    give_far(1)
    arrive(copies)
    total = part[me]
    for d in range(1, count):
        total = total + slots[d]
    whole[me] = total
    copies = stage(2, "cols", me, count, lambda p: whole.at[me], lambda d: whole.at[me])
    give_far(2)
    arrive(copies)
    summed[r] = whole[...]
    arrive(stage(3, "rows", r, split, lambda p: whole, lambda d: summed.at[r]))

    rotate(groups, summed[...].reshape(-1, w), ref["coef"], ref["turn_of"], ref["gram"], ref["turn"])

    segments = []
    for i, (start, stop) in enumerate(near_at):
        segments.append((near[i], start, stop, False))
    for i, (start, stop) in enumerate(far_at):
        segments.append((far[i], start, stop, True))

    def slot(dest):
        found = jnp.int32(0)
        for g in range(groups):
            for i, q in enumerate(quad_blocks(pairing, count, g)):
                found = jnp.where(q == dest, 4 * g + i, found)
        return found

    def place(owner, start, stop):
        return out_ref.at[owner, pl.ds(start, stop - start)]

    def make(dest, number, coef, buffer, first, rows):
        blocks = [buffer[dest, first : first + rows]]
        blocks += [buffer[dest ^ mask, first : first + rows] for mask in masks]
        high, low = halves(jnp.concatenate(blocks, axis=1))
        product = partial(jnp.dot, preferred_element_type=jnp.float32)
        return product(high, coef[0]) + (product(high, coef[1]) + product(low, coef[0]))

    beside_jobs, across_jobs = [], []
    for i, (buffer, start, stop, far_rows) in enumerate(segments):
        beside_jobs.append((i, buffer, 0, start, stop, far_rows))
        if not far_rows and stop > kept:
            first = max(start, kept)
            across_jobs.append((i, buffer, first - start, first, stop, far_rows))

    def emit(index, dest, job, coef):
        i, buffer, first, start, stop, far_rows = job
        piece_ref = ref["piece"].at[index, pl.ds(start + (slab if far_rows else 0), stop - start)]
        piece_ref[...] = make(dest, index, coef, buffer, first, stop - start)
        return piece_ref, place(mirror(me) if far_rows else me, start, stop)

    for i in range(len(EXTRAS)):
        take(len(PARTS) + i, far[i])
    for copy in kept_copies[len(PARTS) :]:
        copy.wait()

    for index, dest in enumerate(others):
        coef = halves(ref["coef"][slot(dest)])
        for job in across_jobs if index < half else beside_jobs:
            src, dst = emit(index, dest, job, coef)
            send(src, dst, ref["back_s"].at[index, job[0]], ref["back_r"].at[me, job[0]], "cols", dest)
    coef = halves(ref["coef"][slot(me)])
    local = []
    for job in beside_jobs:
        src, dst = emit(len(others), me, job, coef)
        local.append(pltpu.make_async_copy(src, dst, ref["home"].at[job[0]]))
        local[-1].start()
    for index, source in enumerate(others):
        for i, _, _, start, stop, far_rows in across_jobs if index < half else beside_jobs:
            dst = place(mirror(source) if far_rows else source, start, stop)
            remote(
                dst, dst, ref["back_s"].at[index, i], ref["back_r"].at[source, i], "cols", source
            ).wait_recv()
    for copy in local:
        copy.wait()
    for copy in sent:
        copy.wait_send()


def rotate(groups, band_ref, coef_ref, turn_ref, gram, turn):
    w = band_ref.shape[1]
    pairs = 2 * groups
    lo, hi = slice(0, w), slice(w, 2 * w)

    def bands(g, i):
        start = (g * PAIRS + i) * 2 * BAND
        return band_ref[start : start + 2 * BAND, :]

    def reset_turns():
        shape = turn.shape
        one = lax.broadcasted_iota(jnp.int32, shape, 1) == BAND
        lower = lax.broadcasted_iota(jnp.int32, shape, 2) >= pairs
        right = lax.broadcasted_iota(jnp.int32, shape, 0) == 1
        turn[...] = jnp.where(one & (lower == right), 1.0, 0.0)

    def put_turns(slot):
        for g in range(groups):
            for p in range(2):
                at = 2 * g + p
                for row, side in ((lo, at), (hi, pairs + at)):
                    turn_ref[g, slot + p, row, lo] = from_bands(turn[0, :, side, :])
                    moved = from_bands(turn[1, :, side, :])
                    turn_ref[g, slot + p, row, hi] = pltpu.roll(moved, SHIFTS, 1)

    def put_gram(at, ll, lr, rl, rr):
        gram[0, :, at, :] = ll
        gram[1, :, at, :] = lr
        gram[0, :, pairs + at, :] = rl
        gram[1, :, pairs + at, :] = rr

    for g in range(groups):
        for p in range(2):
            below = bands(g, 3 * p + 1)
            above = to_bands(from_bands(below).T)
            put_gram(2 * g + p, bands(g, 3 * p), above, below, bands(g, 3 * p + 2))
    reset_turns()
    turn_pairs(gram, turn, pairs)
    put_turns(0)

    for g in range(groups):
        blocks = [from_bands(bands(g, 6 + i)) for i in range(4)]
        cross = jnp.concatenate(
            [
                jnp.concatenate([blocks[0], blocks[1]], axis=1),
                jnp.concatenate([blocks[2], blocks[3]], axis=1),
            ],
            axis=0,
        )
        half = dot(cross, turn_ref[g, 0])
        below = [
            dot_t(turn_ref[g, 1, :, lo], half[:, lo]),
            dot_t(turn_ref[g, 1, :, hi], half[:, hi]),
        ]
        a, b = 2 * g, 2 * g + 1
        a_lo, b_lo = gram[0, :, a, :], gram[0, :, b, :]
        a_hi = pltpu.roll(gram[1, :, pairs + a, :], SHIFTS, 1)
        b_hi = pltpu.roll(gram[1, :, pairs + b, :], SHIFTS, 1)
        put_gram(a, a_lo, to_bands(below[0].T), to_bands(below[0]), b_lo)
        put_gram(b, a_hi, to_bands(below[1].T), to_bands(below[1]), b_hi)
    reset_turns()
    turn_pairs(gram, turn, pairs)
    put_turns(2)

    for g in range(groups):
        for side, part in ((0, lo), (1, hi)):
            last = turn_ref.at[g, 2 + side]
            top = dot(turn_ref[g, 0, :, part], last[lo, :])
            bottom = dot(turn_ref[g, 1, :, part], last[hi, :])
            rows = [top[lo], top[hi], bottom[lo], bottom[hi]]
            for member, cols in ((side, lo), (2 + side, hi)):
                for i in range(4):
                    coef_ref[4 * g + member, i * w : (i + 1) * w, :] = rows[member ^ i][:, cols]


def on_device(anomalies, pairing):
    count, split = lax.axis_size("cols"), lax.axis_size("rows")
    rows, w = anomalies.shape
    slab = rows // count
    unit = slab // UNITS
    groups = count // 4
    f32 = jnp.float32
    block = 8 * split * count
    total = -(-groups * PAIRS * 2 * BAND // block) * block
    piece = total // (split * count)
    extra = sum(EXTRAS) * unit
    segments = len(PARTS) + len(EXTRAS)
    peers = max(count, split)
    dma = pltpu.SemaphoreType.DMA
    scratch = {
        "acc": pltpu.VMEM((groups, 3, 2 * w, 2 * w), f32),
        "bands": pltpu.VMEM((split, total // split // (2 * BAND), 2 * BAND, w), f32),
        "landed": pltpu.VMEM((split, total // split // (2 * BAND), 2 * BAND, w), f32),
        "part": pltpu.VMEM((count, piece, w), f32),
        "slots": pltpu.VMEM((count, piece, w), f32),
        "whole": pltpu.VMEM((count, piece, w), f32),
        "summed": pltpu.VMEM((split, count, piece, w), f32),
        "turn_of": pltpu.VMEM((groups, 4, 2 * w, 2 * w), f32),
        "gram": pltpu.VMEM((2, 2 * BAND, 4 * groups, w), f32),
        "turn": pltpu.VMEM((2, 2 * BAND, 4 * groups, w), f32),
        "coef": pltpu.VMEM((4 * groups, 4 * w, w), f32),
        "piece": pltpu.VMEM((count, slab + extra, w), f32),
        "give": dma((segments, count - 1)),
        "get": dma((segments, count)),
        "own": dma((segments,)),
        "sum_s": dma((4, peers)),
        "sum_r": dma((4, peers)),
        "back_s": dma((count, segments)),
        "back_r": dma((count, segments)),
        "home": dma((segments,)),
    }
    for i, size in enumerate(PARTS):
        scratch["near%d" % i] = pltpu.VMEM((count, size * unit, w), f32)
    for i, size in enumerate(EXTRAS):
        scratch["far%d" % i] = pltpu.VMEM((count, size * unit, w), f32)
    out = pl.pallas_call(
        partial(fused_kernel, count, split, unit, tuple(scratch)),
        out_shape=jax.ShapeDtypeStruct((count, slab, w), f32),
        in_specs=[
            pl.BlockSpec(memory_space=pltpu.SMEM),
            pl.BlockSpec(memory_space=pl.ANY),
        ],
        out_specs=pl.BlockSpec(memory_space=pl.ANY),
        scratch_shapes=list(scratch.values()),
        compiler_params=pltpu.CompilerParams(collective_id=1, has_side_effects=True),
    )(pairing, anomalies.reshape(count, slab, w))
    return out.reshape(rows, w)


def solution(mesh):
    placed = (P("rows", "cols"), P())
    return jax.shard_map(
        on_device, mesh=mesh, in_specs=placed, out_specs=P("rows", "cols"), check_vma=False
    )
```

```python
from functools import partial

import jax
import jax.numpy as jnp
from jax import lax
from jax.experimental import pallas as pl
from jax.experimental.pallas import tpu as pltpu
from jax.sharding import PartitionSpec as P

SHIFTS = 8
TIE_GUARD = 1e-06
BAND = 2 * SHIFTS
PAIRS = 10
MESH = pl.DeviceIdType.MESH
HIGHEST = lax.Precision.HIGHEST
UNITS = 8
PARTS = (3, 3, 1, 1)
EXTRAS = (3, 2, 3)


def dot(left, right):
    return jnp.dot(left, right, precision=HIGHEST, preferred_element_type=jnp.float32)


def dot_t(left, right):
    return lax.dot_general(
        left,
        right,
        (((0,), (0,)), ((), ())),
        precision=HIGHEST,
        preferred_element_type=jnp.float32,
    )


def halves(value):
    high = value.astype(jnp.bfloat16)
    return high, (value - high.astype(jnp.float32)).astype(jnp.bfloat16)


def dot_3(left, right):
    a, b = halves(left)
    c, d = halves(right)
    product = partial(jnp.dot, preferred_element_type=jnp.float32)
    return product(a, c) + (product(a, d) + product(b, c))


def quad_blocks(pairing, count, g):
    m0 = pairing[0, 0]
    m1 = pairing[1, 0]
    lower_mask = jnp.minimum(m0, m1)
    low_bits = jnp.int32(0)
    for bit in range(1, count.bit_length() - 1):
        low_bits = jnp.where(lower_mask >= (1 << bit), (1 << bit) - 1, low_bits)
    rest = g & low_bits
    q0 = rest + 2 * (g - rest)
    return q0, q0 ^ m0, q0 ^ m1, q0 ^ (count - 1)


def lane_bit(shape, bit):
    return (lax.broadcasted_iota(jnp.int32, shape, 1) & (1 << bit)) != 0


def to_bands(block):
    w = block.shape[0]
    for bit in range(w.bit_length() - 1):
        block = jnp.where(
            lane_bit(block.shape, bit), pltpu.roll(block, w - (1 << bit), 0), block
        )
    return jnp.concatenate([block[w - BAND :], block[:BAND]], axis=0)


def from_bands(bands):
    w = bands.shape[1]
    block = jnp.concatenate(
        [bands[BAND:], jnp.zeros((w - 2 * BAND, w), jnp.float32), bands[:BAND]], axis=0
    )
    for bit in range(w.bit_length() - 1):
        block = jnp.where(lane_bit(block.shape, bit), pltpu.roll(block, 1 << bit, 0), block)
    return block


def turn_pairs(gram, turn, pairs):
    _, depth, sides, w = gram.shape

    def lane(value):
        return pltpu.roll(value.reshape(depth * sides, w), w - 1, 1).reshape(depth, sides, w)

    def later(value):
        return jnp.concatenate([value[-1:], value[:-1]], axis=0)

    def sooner(value):
        return jnp.concatenate([value[1:], value[:1]], axis=0)

    def swap(value):
        return jnp.concatenate([value[:, pairs:], value[:, :pairs]], axis=1)

    def ahead(value):
        return jnp.stack([pltpu.roll(value, (BAND - r) % w, 1) if r != BAND else value for r in range(depth)])

    lower = lax.broadcasted_iota(jnp.int32, (depth, sides, w), 1) >= pairs

    @pl.loop(0, SHIFTS)
    def _(step):
        g_l, g_r = gram[0], gram[1]
        a, e, g = gram[0, BAND, :pairs], gram[1, BAND, pairs:], gram[1, BAND, :pairs]
        gap = e - a
        sign = jnp.where(gap >= 0.0, 1.0, -1.0)
        denom = jnp.abs(gap) + jnp.sqrt(gap * gap + 4.0 * g * g) + TIE_GUARD * (a + e)
        tangent = 2.0 * g * sign / denom
        cosine = 1.0 / jnp.sqrt(1.0 + tangent * tangent)
        sine = cosine * tangent
        c_2 = jnp.concatenate([cosine, cosine], axis=0)
        s_2 = jnp.concatenate([sine, sine], axis=0)
        c_d = ahead(c_2)
        s_d = ahead(jnp.concatenate([-sine, sine], axis=0))
        t_l = g_l * c_2 - g_r * s_2
        t_r = g_l * s_2 + g_r * c_2
        t_l = c_d * t_l + s_d * swap(t_l)
        t_r = lane(c_d * t_r + s_d * swap(t_r))
        gram[0] = jnp.where(lower, sooner(t_l), t_l)
        gram[1] = jnp.where(lower, t_r, later(t_r))
        v_l, v_r = turn[0], turn[1]
        turn[0] = v_l * c_2 - v_r * s_2
        turn[1] = later(lane(v_l * s_2 + v_r * c_2))


def spans(sizes, unit):
    out, at = [], 0
    for size in sizes:
        out.append((at * unit, (at + size) * unit))
        at += size
    return out


def fused_kernel(count, split, unit, names, pairing, x_ref, out_ref, *refs):
    ref = dict(zip(names, refs))
    near = [ref["near%d" % i] for i in range(len(PARTS))]
    far = [ref["far%d" % i] for i in range(len(EXTRAS))]
    near_at, far_at = spans(PARTS, unit), spans(EXTRAS, unit)
    slab, kept = UNITS * unit, sum(EXTRAS) * unit
    half, groups = count // 2, count // 4
    w = x_ref.shape[2]
    lo, hi = slice(0, w), slice(w, 2 * w)
    me, r = lax.axis_index("cols"), lax.axis_index("rows")
    side, pos = me // half, me % half
    across = [(1 - side) * half + (pos + j) % half for j in range(half)]
    beside = [side * half + (pos + j) % half for j in range(1, half)]
    others = across + beside
    ends = [0, 1, count - 2, count - 1]
    masks = (pairing[0, 0], pairing[1, 0], count - 1)

    def at_end(d):
        return (d < 2) | (d >= count - 2)

    def mirror(d):
        return count - 1 - d

    barrier = pltpu.get_barrier_semaphore()
    for dest in others:
        pl.semaphore_signal(barrier, inc=1, device_id={"cols": dest}, device_id_type=MESH)
    for d in range(1, split):
        pl.semaphore_signal(
            barrier, inc=1, device_id={"rows": (r + d) % split}, device_id_type=MESH
        )
    pl.semaphore_wait(barrier, count + split - 2)

    def remote(src, dst, send, recv, axis, peer):
        return pltpu.make_async_remote_copy(
            src_ref=src,
            dst_ref=dst,
            send_sem=send,
            recv_sem=recv,
            device_id={axis: peer},
            device_id_type=MESH,
        )

    sent = []

    def send(*args, when=None):
        copy = remote(*args)
        sent.append((copy, when))
        if when is None:
            copy.start()
        else:
            pl.when(when)(copy.start)

    def keep(number, land, at, owner):
        rows = pl.ds(at[0], at[1] - at[0])
        return pltpu.make_async_copy(x_ref.at[owner, rows], land.at[me], ref["own"].at[number])

    def give_near(i):
        rows = pl.ds(near_at[i][0], near_at[i][1] - near_at[i][0])
        for n, dest in enumerate(others):
            send(x_ref.at[dest, rows], near[i].at[me], ref["give"].at[i, n], ref["get"].at[i, me], "cols", dest)

    def give_far(i, crossing):
        rows = pl.ds(far_at[i][0], far_at[i][1] - far_at[i][0])
        n = len(PARTS) + i
        for k, dest in enumerate(ends):
            cross = (dest // half) != side
            when = cross if crossing else jnp.logical_not(cross) & (dest != me)
            send(x_ref.at[mirror(dest), rows], far[i].at[me], ref["give_s"].at[i, k], ref["get"].at[n, me], "cols", dest, when=when)

    def take(number, land):
        for source in others:
            remote(
                land.at[source], land.at[source], ref["give"].at[0, 0], ref["get"].at[number, source], "cols", source
            ).wait_recv()

    near_keep = [keep(i, near[i], at, me) for i, at in enumerate(near_at)]
    far_keep = [keep(len(PARTS) + i, far[i], at, mirror(me)) for i, at in enumerate(far_at)]
    for copy in near_keep:
        copy.start()
    for copy in far_keep:
        pl.when(at_end(me))(copy.start)
    for i in range(len(PARTS)):
        give_near(i)
    for i in range(len(EXTRAS)):
        give_far(i, False)
    give_far(0, True)

    acc, bands = ref["acc"], ref["bands"]
    for i, land in enumerate(near):
        near_keep[i].wait()
        take(i, land)
        for g in range(groups):
            x = [land[q] for q in quad_blocks(pairing, count, g)]
            a = jnp.concatenate(x[:2], axis=1)
            b = jnp.concatenate(x[2:], axis=1)
            for k, block in enumerate((dot_t(a, a), dot_t(b, b), dot_t(b, a))):
                acc[g, k] = block if i == 0 else acc[g, k] + block
    places = [(0, lo, lo), (0, hi, lo), (0, hi, hi), (1, lo, lo), (1, hi, lo), (1, hi, hi)]
    places += [(2, lo, lo), (2, lo, hi), (2, hi, lo), (2, hi, hi)]
    for g in range(groups):
        for i, (k, rows, cols) in enumerate(places):
            first, size = band_place(g, i)
            bands[first : first + size] = to_bands(acc[g, k, rows, cols])[2 * BAND - size :]

    landed, slots, part, summed = (ref[n] for n in ("landed", "slots", "part", "summed"))
    piece = slots.shape[1]

    def at(row, col):
        return pl.ds(pl.multiple_of((row * count + col) * piece, piece), piece)

    for k, c in enumerate(others + [me]):
        for d in range(1, split):
            peer = (r + d) % split
            send(bands.at[at(peer, c)], landed.at[d, k], ref["rs_s"].at[d, k], ref["rs_r"].at[d, k], "rows", peer)
    for k, c in enumerate(others + [me]):
        total = bands[at(r, c)]
        for d in range(1, split):
            peer = (r + split - d) % split
            remote(landed.at[d, k], landed.at[d, k], ref["rs_s"].at[d, k], ref["rs_r"].at[d, k], "rows", peer).wait_recv()
            total = total + landed[d, k]
        part[k] = total
        if k < len(others):
            send(part.at[k], slots.at[me], ref["sum_s"].at[0, k], ref["sum_r"].at[0, me], "cols", c)
    give_far(1, True)
    for c in others:
        remote(slots.at[c], slots.at[c], ref["sum_s"].at[0, 0], ref["sum_r"].at[0, c], "cols", c).wait_recv()
        total = total + slots[c]
    summed[at(r, me)] = total
    mine = summed.at[at(r, me)]

    def spread(source, k):
        for d in range(1, split):
            peer = (r + d) % split
            block = summed.at[at(r, source)]
            send(block, block, ref["ag_s"].at[d, k], ref["ag_r"].at[r, k], "rows", peer)

    for k, c in enumerate(others):
        send(mine, mine, ref["sum_s"].at[1, k], ref["sum_r"].at[1, me], "cols", c)
    spread(me, len(others))
    give_far(2, True)
    for k, c in reversed(list(enumerate(others))):
        block = summed.at[at(r, c)]
        remote(block, block, ref["sum_s"].at[1, k], ref["sum_r"].at[1, c], "cols", c).wait_recv()
        spread(c, k)
    for d in range(1, split):
        row = (r + d) % split
        for k, c in enumerate(others + [me]):
            block = summed.at[at(row, c)]
            remote(block, block, ref["ag_s"].at[d, k], ref["ag_r"].at[row, k], "rows", row).wait_recv()

    rotate(groups, summed, ref["coef"], ref["turn_of"], ref["gram"], ref["turn"])

    def slot(dest):
        found = jnp.int32(0)
        for g in range(groups):
            for i, q in enumerate(quad_blocks(pairing, count, g)):
                found = jnp.where(q == dest, 4 * g + i, found)
        return found

    def make(dest, coef, buffer):
        blocks = [buffer[dest]] + [buffer[dest ^ mask] for mask in masks]
        high, low = halves(jnp.concatenate(blocks, axis=1))
        product = partial(jnp.dot, preferred_element_type=jnp.float32)
        return product(high, coef[0]) + (product(high, coef[1]) + product(low, coef[0]))

    def place(owner, at):
        return out_ref.at[owner, pl.ds(at[0], at[1] - at[0])]

    end = at_end(me)
    inner = jnp.logical_not(end)
    jobs = [(i, near[i], at, False) for i, at in enumerate(near_at)]
    jobs += [(len(PARTS) + i, far[i], at, True) for i, at in enumerate(far_at)]

    def when_of(job, crossing, whose):
        _, _, at, is_far = job
        if is_far:
            return False if crossing else at_end(whose)
        if crossing and at[0] < kept:
            return jnp.logical_not(at_end(whose))
        return None

    def emit(n, dest, job):
        number, buffer, at, is_far = job
        when = when_of(job, n < half, me)
        if when is False:
            return
        base = slab if is_far else 0
        src = ref["piece"].at[n, pl.ds(base + at[0], at[1] - at[0])]

        def fill():
            src[...] = make(dest, halves(ref["coef"][slot(dest)]), buffer)

        if when is None:
            fill()
        else:
            pl.when(when)(fill)
        dst = place(mirror(me) if is_far else me, at)
        send(src, dst, ref["back_s"].at[n, number], ref["back_r"].at[me, number], "cols", dest, when=when)

    for job in jobs:
        i = job[0] - len(PARTS)
        if i == 0:
            for k in range(len(EXTRAS)):
                pl.when(end)(partial(take, len(PARTS) + k, far[k]))
                pl.when(end)(far_keep[k].wait)
        for n, dest in enumerate(others):
            emit(n, dest, job)
    for number, buffer, at, is_far in jobs:

        def fill(buffer=buffer, at=at, is_far=is_far):
            place(mirror(me) if is_far else me, at)[...] = make(me, halves(ref["coef"][slot(me)]), buffer)

        if is_far:
            pl.when(end)(fill)
        else:
            fill()
    for n, source in enumerate(others):
        for job in jobs:
            when = when_of(job, n < half, source)
            if when is False:
                continue
            dst = place(mirror(source) if job[3] else source, job[2])
            copy = remote(dst, dst, ref["back_s"].at[n, job[0]], ref["back_r"].at[source, job[0]], "cols", source)
            if when is None:
                copy.wait_recv()
            else:
                pl.when(when)(copy.wait_recv)
    for copy, when in sent:
        if when is None:
            copy.wait_send()
        else:
            pl.when(when)(copy.wait_send)


def band_place(g, i):
    sizes = [BAND, 2 * BAND, BAND, BAND, 2 * BAND, BAND] + [2 * BAND] * 4
    return g * sum(sizes) + sum(sizes[:i]), sizes[i]


def rotate(groups, band_ref, coef_ref, turn_ref, gram, turn):
    w = band_ref.shape[1]
    pairs = 2 * groups
    lo, hi = slice(0, w), slice(w, 2 * w)

    def bands(g, i):
        start, size = band_place(g, i)
        return band_ref[start : start + size, :]

    def reset_turns():
        shape = turn.shape
        one = lax.broadcasted_iota(jnp.int32, shape, 1) == BAND
        lower = lax.broadcasted_iota(jnp.int32, shape, 2) >= pairs
        right = lax.broadcasted_iota(jnp.int32, shape, 0) == 1
        turn[...] = jnp.where(one & (lower == right), 1.0, 0.0)

    def put_turns(slot):
        for g in range(groups):
            for p in range(2):
                at = 2 * g + p
                for row, side in ((lo, at), (hi, pairs + at)):
                    turn_ref[g, slot + p, row, lo] = from_bands(turn[0, :, side, :])
                    moved = from_bands(turn[1, :, side, :])
                    turn_ref[g, slot + p, row, hi] = pltpu.roll(moved, SHIFTS, 1)

    def put_gram(at, ll, lr, rl, rr):
        gram[0, :, at, :] = ll
        gram[1, :, at, :] = lr
        gram[0, :, pairs + at, :] = rl
        gram[1, :, pairs + at, :] = rr

    for g in range(groups):
        for p in range(2):
            at = 2 * g + p
            below = bands(g, 3 * p + 1)
            gram[0, BAND:, at, :] = bands(g, 3 * p)
            gram[1, :, at, :] = to_bands(from_bands(below).T)
            gram[0, :, pairs + at, :] = below
            gram[1, BAND:, pairs + at, :] = bands(g, 3 * p + 2)
    for k, sides in ((0, slice(0, pairs)), (1, slice(pairs, 2 * pairs))):
        gram[k, 0, sides, :] = jnp.zeros((pairs, w), jnp.float32)
        for d in range(1, BAND):
            gram[k, BAND - d, sides, :] = pltpu.roll(gram[k, BAND + d, sides, :], d, 1)
    reset_turns()
    turn_pairs(gram, turn, pairs)
    put_turns(0)

    for g in range(groups):
        blocks = [from_bands(bands(g, 6 + i)) for i in range(4)]
        cross = jnp.concatenate(
            [
                jnp.concatenate([blocks[0], blocks[1]], axis=1),
                jnp.concatenate([blocks[2], blocks[3]], axis=1),
            ],
            axis=0,
        )
        half = dot(cross, turn_ref[g, 0])
        below = [
            dot_t(turn_ref[g, 1, :, lo], half[:, lo]),
            dot_t(turn_ref[g, 1, :, hi], half[:, hi]),
        ]
        a, b = 2 * g, 2 * g + 1
        a_lo, b_lo = gram[0, :, a, :], gram[0, :, b, :]
        a_hi = pltpu.roll(gram[1, :, pairs + a, :], SHIFTS, 1)
        b_hi = pltpu.roll(gram[1, :, pairs + b, :], SHIFTS, 1)
        put_gram(a, a_lo, to_bands(below[0].T), to_bands(below[0]), b_lo)
        put_gram(b, a_hi, to_bands(below[1].T), to_bands(below[1]), b_hi)
    reset_turns()
    turn_pairs(gram, turn, pairs)
    put_turns(2)

    for g in range(groups):
        for side, part in ((0, lo), (1, hi)):
            last = turn_ref.at[g, 2 + side]
            top = dot(turn_ref[g, 0, :, part], last[lo, :])
            bottom = dot(turn_ref[g, 1, :, part], last[hi, :])
            rows = [top[lo], top[hi], bottom[lo], bottom[hi]]
            for member, cols in ((side, lo), (2 + side, hi)):
                for i in range(4):
                    coef_ref[4 * g + member, i * w : (i + 1) * w, :] = rows[member ^ i][:, cols]


def on_device(anomalies, pairing):
    count, split = lax.axis_size("cols"), lax.axis_size("rows")
    rows, w = anomalies.shape
    slab = rows // count
    unit = slab // UNITS
    groups = count // 4
    f32 = jnp.float32
    block = 8 * split * count
    total = -(-band_place(groups, 0)[0] // block) * block
    piece = total // (split * count)
    extra = sum(EXTRAS) * unit
    segments = len(PARTS) + len(EXTRAS)
    dma = pltpu.SemaphoreType.DMA
    scratch = {
        "acc": pltpu.VMEM((groups, 3, 2 * w, 2 * w), f32),
        "bands": pltpu.VMEM((total, w), f32),
        "landed": pltpu.VMEM((split, count, piece, w), f32),
        "part": pltpu.VMEM((count, piece, w), f32),
        "slots": pltpu.VMEM((count, piece, w), f32),
        "summed": pltpu.VMEM((total, w), f32),
        "turn_of": pltpu.VMEM((groups, 4, 2 * w, 2 * w), f32),
        "gram": pltpu.VMEM((2, 2 * BAND, 4 * groups, w), f32),
        "turn": pltpu.VMEM((2, 2 * BAND, 4 * groups, w), f32),
        "coef": pltpu.VMEM((4 * groups, 4 * w, w), f32),
        "piece": pltpu.VMEM((count - 1, slab + extra, w), f32),
        "give": dma((len(PARTS), count - 1)),
        "give_s": dma((len(EXTRAS), 4)),
        "get": dma((segments, count)),
        "own": dma((segments,)),
        "rs_s": dma((split, count)),
        "rs_r": dma((split, count)),
        "ag_s": dma((split, count)),
        "ag_r": dma((split, count)),
        "sum_s": dma((2, count)),
        "sum_r": dma((2, count)),
        "back_s": dma((count, segments)),
        "back_r": dma((count, segments)),
    }
    for i, size in enumerate(PARTS):
        scratch["near%d" % i] = pltpu.VMEM((count, size * unit, w), f32)
    for i, size in enumerate(EXTRAS):
        scratch["far%d" % i] = pltpu.VMEM((count, size * unit, w), f32)
    out = pl.pallas_call(
        partial(fused_kernel, count, split, unit, tuple(scratch)),
        out_shape=pltpu.VMEM((count, slab, w), f32),
        in_specs=[
            pl.BlockSpec(memory_space=pltpu.SMEM),
            pl.BlockSpec(memory_space=pl.ANY),
        ],
        out_specs=pl.BlockSpec(memory_space=pltpu.VMEM),
        scratch_shapes=list(scratch.values()),
        compiler_params=pltpu.CompilerParams(collective_id=1, has_side_effects=True),
    )(pairing, anomalies.reshape(count, slab, w))
    return out.reshape(rows, w)


def solution(mesh):
    placed = (P("rows", "cols"), P())
    return jax.shard_map(
        on_device, mesh=mesh, in_specs=placed, out_specs=P("rows", "cols"), check_vma=False
    )
```

```python
from functools import partial

import jax
import jax.numpy as jnp
from jax import lax
from jax.experimental import pallas as pl
from jax.experimental.pallas import tpu as pltpu
from jax.sharding import PartitionSpec as P

SHIFTS = 8
TIE_GUARD = 1e-06
BAND = 2 * SHIFTS
PAIRS = 10
MESH = pl.DeviceIdType.MESH
HIGHEST = lax.Precision.HIGHEST
UNITS = 8
PARTS = (3, 3, 1, 1)
EXTRAS = (1, 1, 6)
POINTS = (0, 2, 3)


def dot(left, right):
    return jnp.dot(left, right, precision=HIGHEST, preferred_element_type=jnp.float32)


def dot_t(left, right):
    return lax.dot_general(
        left,
        right,
        (((0,), (0,)), ((), ())),
        precision=HIGHEST,
        preferred_element_type=jnp.float32,
    )


def halves(value):
    high = value.astype(jnp.bfloat16)
    return high, (value - high.astype(jnp.float32)).astype(jnp.bfloat16)


def dot_3(left, right):
    a, b = halves(left)
    c, d = halves(right)
    product = partial(jnp.dot, preferred_element_type=jnp.float32)
    return product(a, c) + (product(a, d) + product(b, c))


def quad_blocks(pairing, count, g):
    m0 = pairing[0, 0]
    m1 = pairing[1, 0]
    lower_mask = jnp.minimum(m0, m1)
    low_bits = jnp.int32(0)
    for bit in range(1, count.bit_length() - 1):
        low_bits = jnp.where(lower_mask >= (1 << bit), (1 << bit) - 1, low_bits)
    rest = g & low_bits
    q0 = rest + 2 * (g - rest)
    return q0, q0 ^ m0, q0 ^ m1, q0 ^ (count - 1)


def lane_bit(shape, bit):
    return (lax.broadcasted_iota(jnp.int32, shape, 1) & (1 << bit)) != 0


def to_bands(block):
    w = block.shape[0]
    for bit in range(w.bit_length() - 1):
        block = jnp.where(
            lane_bit(block.shape, bit), pltpu.roll(block, w - (1 << bit), 0), block
        )
    return jnp.concatenate([block[w - BAND :], block[:BAND]], axis=0)


def from_bands(bands):
    w = bands.shape[1]
    block = jnp.concatenate(
        [bands[BAND:], jnp.zeros((w - 2 * BAND, w), jnp.float32), bands[:BAND]], axis=0
    )
    for bit in range(w.bit_length() - 1):
        block = jnp.where(lane_bit(block.shape, bit), pltpu.roll(block, 1 << bit, 0), block)
    return block


def turn_pairs(gram, turn, pairs):
    _, depth, sides, w = gram.shape

    def lane(value):
        return pltpu.roll(value.reshape(depth * sides, w), w - 1, 1).reshape(depth, sides, w)

    def later(value):
        return jnp.concatenate([value[-1:], value[:-1]], axis=0)

    def sooner(value):
        return jnp.concatenate([value[1:], value[:1]], axis=0)

    def swap(value):
        return jnp.concatenate([value[:, pairs:], value[:, :pairs]], axis=1)

    def ahead(value):
        return jnp.stack([pltpu.roll(value, (BAND - r) % w, 1) if r != BAND else value for r in range(depth)])

    lower = lax.broadcasted_iota(jnp.int32, (depth, sides, w), 1) >= pairs

    @pl.loop(0, SHIFTS)
    def _(step):
        g_l, g_r = gram[0], gram[1]
        a, e, g = gram[0, BAND, :pairs], gram[1, BAND, pairs:], gram[1, BAND, :pairs]
        gap = e - a
        sign = jnp.where(gap >= 0.0, 1.0, -1.0)
        denom = jnp.abs(gap) + jnp.sqrt(gap * gap + 4.0 * g * g) + TIE_GUARD * (a + e)
        tangent = 2.0 * g * sign / denom
        cosine = 1.0 / jnp.sqrt(1.0 + tangent * tangent)
        sine = cosine * tangent
        c_2 = jnp.concatenate([cosine, cosine], axis=0)
        s_2 = jnp.concatenate([sine, sine], axis=0)
        c_d = ahead(c_2)
        s_d = ahead(jnp.concatenate([-sine, sine], axis=0))
        t_l = g_l * c_2 - g_r * s_2
        t_r = g_l * s_2 + g_r * c_2
        t_l = c_d * t_l + s_d * swap(t_l)
        t_r = lane(c_d * t_r + s_d * swap(t_r))
        gram[0] = jnp.where(lower, sooner(t_l), t_l)
        gram[1] = jnp.where(lower, t_r, later(t_r))
        v_l, v_r = turn[0], turn[1]
        turn[0] = v_l * c_2 - v_r * s_2
        turn[1] = later(lane(v_l * s_2 + v_r * c_2))


def spans(sizes, unit):
    out, at = [], 0
    for size in sizes:
        out.append((at * unit, (at + size) * unit))
        at += size
    return out


def fused_kernel(count, split, unit, names, pairing, x_ref, out_ref, *refs):
    ref = dict(zip(names, refs))
    near = [ref["near%d" % i] for i in range(len(PARTS))]
    far = [ref["far%d" % i] for i in range(len(EXTRAS))]
    near_at, far_at = spans(PARTS, unit), spans(EXTRAS, unit)
    slab, kept = UNITS * unit, sum(EXTRAS) * unit
    half, groups = count // 2, count // 4
    w = x_ref.shape[2]
    lo, hi = slice(0, w), slice(w, 2 * w)
    me, r = lax.axis_index("cols"), lax.axis_index("rows")
    side, pos = me // half, me % half
    across = [(1 - side) * half + (pos + j) % half for j in range(half)]
    beside = [side * half + (pos + j) % half for j in range(1, half)]
    others = across + beside
    masks = (pairing[0, 0], pairing[1, 0], count - 1)

    def at_end(d):
        return (d < 2) | (d >= count - 2)

    def mirror(d):
        return count - 1 - d

    barrier = pltpu.get_barrier_semaphore()
    for dest in others:
        pl.semaphore_signal(barrier, inc=1, device_id={"cols": dest}, device_id_type=MESH)
    for d in range(1, split):
        pl.semaphore_signal(
            barrier, inc=1, device_id={"rows": (r + d) % split}, device_id_type=MESH
        )
    pl.semaphore_wait(barrier, count + split - 2)

    def remote(src, dst, send, recv, axis, peer):
        return pltpu.make_async_remote_copy(
            src_ref=src,
            dst_ref=dst,
            send_sem=send,
            recv_sem=recv,
            device_id={axis: peer},
            device_id_type=MESH,
        )

    sent = []

    def send(*args, when=None):
        copy = remote(*args)
        sent.append((copy, when))
        if when is None:
            copy.start()
        else:
            pl.when(when)(copy.start)

    def keep(number, land, at, owner):
        rows = pl.ds(at[0], at[1] - at[0])
        return pltpu.make_async_copy(x_ref.at[owner, rows], land.at[me], ref["own"].at[number])

    def give_near(i):
        rows = pl.ds(near_at[i][0], near_at[i][1] - near_at[i][0])
        for n, dest in enumerate(others):
            send(x_ref.at[dest, rows], near[i].at[me], ref["give"].at[i, n], ref["get"].at[i, me], "cols", dest)

    def give_far(i, crossing):
        rows = pl.ds(far_at[i][0], far_at[i][1] - far_at[i][0])
        n = len(PARTS) + i
        base = (1 - side if crossing else side) * (count - 2)
        for e in range(2):
            dest = base + (me + e) % 2
            k = e if crossing else 2 + e
            when = None if crossing else dest != me
            send(x_ref.at[mirror(dest), rows], far[i].at[me], ref["give_s"].at[i, k], ref["get"].at[n, me], "cols", dest, when=when)

    def advance(point):
        for i, when in enumerate(POINTS):
            if when == point:
                give_far(i, True)

    def take(number, land):
        for source in others:
            remote(
                land.at[source], land.at[source], ref["give"].at[0, 0], ref["get"].at[number, source], "cols", source
            ).wait_recv()

    near_keep = [keep(i, near[i], at, me) for i, at in enumerate(near_at)]
    far_keep = [keep(len(PARTS) + i, far[i], at, mirror(me)) for i, at in enumerate(far_at)]
    for copy in near_keep:
        copy.start()
    for copy in far_keep:
        pl.when(at_end(me))(copy.start)
    for i in range(len(PARTS)):
        give_near(i)

    for e in range(len(EXTRAS)):
        give_far(e, False)

    acc, bands = ref["acc"], ref["bands"]
    for i, land in enumerate(near):
        near_keep[i].wait()
        take(i, land)
        if i == len(near) - 1:
            advance(0)
        for g in range(groups):
            x = [land[q] for q in quad_blocks(pairing, count, g)]
            a = jnp.concatenate(x[:2], axis=1)
            b = jnp.concatenate(x[2:], axis=1)
            for k, block in enumerate((dot_t(a, a), dot_t(b, b), dot_t(b, a))):
                acc[g, k] = block if i == 0 else acc[g, k] + block
    places = [(0, lo, lo), (0, hi, lo), (0, hi, hi), (1, lo, lo), (1, hi, lo), (1, hi, hi)]
    places += [(2, lo, lo), (2, lo, hi), (2, hi, lo), (2, hi, hi)]
    for g in range(groups):
        for i, (k, rows, cols) in enumerate(places):
            first, size = band_place(g, i)
            bands[first : first + size] = to_bands(acc[g, k, rows, cols])[2 * BAND - size :]

    landed, slots, part, summed = (ref[n] for n in ("landed", "slots", "part", "summed"))
    piece = slots.shape[1]

    def at(row, col):
        return pl.ds(pl.multiple_of((row * count + col) * piece, piece), piece)

    for k, c in enumerate(others + [me]):
        for d in range(1, split):
            peer = (r + d) % split
            send(bands.at[at(peer, c)], landed.at[d, k], ref["rs_s"].at[d, k], ref["rs_r"].at[d, k], "rows", peer)
    advance(1)
    for k, c in enumerate(others + [me]):
        total = bands[at(r, c)]
        for d in range(1, split):
            peer = (r + split - d) % split
            remote(landed.at[d, k], landed.at[d, k], ref["rs_s"].at[d, k], ref["rs_r"].at[d, k], "rows", peer).wait_recv()
            total = total + landed[d, k]
        part[k] = total
        if k < len(others):
            send(part.at[k], slots.at[me], ref["sum_s"].at[0, k], ref["sum_r"].at[0, me], "cols", c)
    advance(2)
    for c in others:
        remote(slots.at[c], slots.at[c], ref["sum_s"].at[0, 0], ref["sum_r"].at[0, c], "cols", c).wait_recv()
        total = total + slots[c]
    summed[at(r, me)] = total
    mine = summed.at[at(r, me)]

    def spread(source, k):
        for d in range(1, split):
            peer = (r + d) % split
            block = summed.at[at(r, source)]
            send(block, block, ref["ag_s"].at[d, k], ref["ag_r"].at[r, k], "rows", peer)

    for k, c in enumerate(others):
        send(mine, mine, ref["sum_s"].at[1, k], ref["sum_r"].at[1, me], "cols", c)
    spread(me, len(others))
    advance(3)
    for k, c in reversed(list(enumerate(others))):
        block = summed.at[at(r, c)]
        remote(block, block, ref["sum_s"].at[1, k], ref["sum_r"].at[1, c], "cols", c).wait_recv()
        spread(c, k)
    advance(4)
    for d in range(1, split):
        row = (r + d) % split
        for k, c in enumerate(others + [me]):
            block = summed.at[at(row, c)]
            remote(block, block, ref["ag_s"].at[d, k], ref["ag_r"].at[row, k], "rows", row).wait_recv()

    rotate(groups, summed, ref["coef"], ref["turn_of"], ref["gram"], ref["turn"])

    def slot(dest):
        found = jnp.int32(0)
        for g in range(groups):
            for i, q in enumerate(quad_blocks(pairing, count, g)):
                found = jnp.where(q == dest, 4 * g + i, found)
        return found

    def make(dest, coef, buffer):
        blocks = [buffer[dest]] + [buffer[dest ^ mask] for mask in masks]
        high, low = halves(jnp.concatenate(blocks, axis=1))
        product = partial(jnp.dot, preferred_element_type=jnp.float32)
        return product(high, coef[0]) + (product(high, coef[1]) + product(low, coef[0]))

    def place(owner, at):
        return out_ref.at[owner, pl.ds(at[0], at[1] - at[0])]

    end = at_end(me)
    inner = jnp.logical_not(end)
    jobs = [(i, near[i], at, False) for i, at in enumerate(near_at)]
    jobs += [(len(PARTS) + i, far[i], at, True) for i, at in enumerate(far_at)]

    def when_of(job, crossing, whose):
        _, _, at, is_far = job
        if is_far:
            return False if crossing else at_end(whose)
        if crossing and at[0] < kept:
            return jnp.logical_not(at_end(whose))
        return None

    def emit(n, dest, job):
        number, buffer, at, is_far = job
        when = when_of(job, n < half, me)
        if when is False:
            return
        base = slab if is_far else 0
        src = ref["piece"].at[n, pl.ds(base + at[0], at[1] - at[0])]

        def fill():
            src[...] = make(dest, halves(ref["coef"][slot(dest)]), buffer)

        if when is None:
            fill()
        else:
            pl.when(when)(fill)
        dst = place(mirror(me) if is_far else me, at)
        send(src, dst, ref["back_s"].at[n, number], ref["back_r"].at[me, number], "cols", dest, when=when)

    for job in jobs:
        i = job[0] - len(PARTS)
        if i == 0:
            for k in range(len(EXTRAS)):
                pl.when(end)(partial(take, len(PARTS) + k, far[k]))
                pl.when(end)(far_keep[k].wait)
        for n, dest in enumerate(others):
            emit(n, dest, job)
    for number, buffer, at, is_far in jobs:

        def fill(buffer=buffer, at=at, is_far=is_far):
            place(mirror(me) if is_far else me, at)[...] = make(me, halves(ref["coef"][slot(me)]), buffer)

        if is_far:
            pl.when(end)(fill)
        else:
            fill()
    for n, source in enumerate(others):
        for job in jobs:
            when = when_of(job, n < half, source)
            if when is False:
                continue
            dst = place(mirror(source) if job[3] else source, job[2])
            copy = remote(dst, dst, ref["back_s"].at[n, job[0]], ref["back_r"].at[source, job[0]], "cols", source)
            if when is None:
                copy.wait_recv()
            else:
                pl.when(when)(copy.wait_recv)
    for copy, when in sent:
        if when is None:
            copy.wait_send()
        else:
            pl.when(when)(copy.wait_send)


def band_place(g, i):
    sizes = [BAND, 2 * BAND, BAND, BAND, 2 * BAND, BAND] + [2 * BAND] * 4
    return g * sum(sizes) + sum(sizes[:i]), sizes[i]


def rotate(groups, band_ref, coef_ref, turn_ref, gram, turn):
    w = band_ref.shape[1]
    pairs = 2 * groups
    lo, hi = slice(0, w), slice(w, 2 * w)

    def bands(g, i):
        start, size = band_place(g, i)
        return band_ref[start : start + size, :]

    def reset_turns():
        shape = turn.shape
        one = lax.broadcasted_iota(jnp.int32, shape, 1) == BAND
        lower = lax.broadcasted_iota(jnp.int32, shape, 2) >= pairs
        right = lax.broadcasted_iota(jnp.int32, shape, 0) == 1
        turn[...] = jnp.where(one & (lower == right), 1.0, 0.0)

    def put_turns(slot):
        for g in range(groups):
            for p in range(2):
                at = 2 * g + p
                for row, side in ((lo, at), (hi, pairs + at)):
                    turn_ref[g, slot + p, row, lo] = from_bands(turn[0, :, side, :])
                    moved = from_bands(turn[1, :, side, :])
                    turn_ref[g, slot + p, row, hi] = pltpu.roll(moved, SHIFTS, 1)

    def put_gram(at, ll, lr, rl, rr):
        gram[0, :, at, :] = ll
        gram[1, :, at, :] = lr
        gram[0, :, pairs + at, :] = rl
        gram[1, :, pairs + at, :] = rr

    for g in range(groups):
        for p in range(2):
            at = 2 * g + p
            below = bands(g, 3 * p + 1)
            gram[0, BAND:, at, :] = bands(g, 3 * p)
            gram[1, :, at, :] = to_bands(from_bands(below).T)
            gram[0, :, pairs + at, :] = below
            gram[1, BAND:, pairs + at, :] = bands(g, 3 * p + 2)
    for k, sides in ((0, slice(0, pairs)), (1, slice(pairs, 2 * pairs))):
        gram[k, 0, sides, :] = jnp.zeros((pairs, w), jnp.float32)
        for d in range(1, BAND):
            gram[k, BAND - d, sides, :] = pltpu.roll(gram[k, BAND + d, sides, :], d, 1)
    reset_turns()
    turn_pairs(gram, turn, pairs)
    put_turns(0)

    for g in range(groups):
        blocks = [from_bands(bands(g, 6 + i)) for i in range(4)]
        cross = jnp.concatenate(
            [
                jnp.concatenate([blocks[0], blocks[1]], axis=1),
                jnp.concatenate([blocks[2], blocks[3]], axis=1),
            ],
            axis=0,
        )
        half = dot(cross, turn_ref[g, 0])
        below = [
            dot_t(turn_ref[g, 1, :, lo], half[:, lo]),
            dot_t(turn_ref[g, 1, :, hi], half[:, hi]),
        ]
        a, b = 2 * g, 2 * g + 1
        a_lo, b_lo = gram[0, :, a, :], gram[0, :, b, :]
        a_hi = pltpu.roll(gram[1, :, pairs + a, :], SHIFTS, 1)
        b_hi = pltpu.roll(gram[1, :, pairs + b, :], SHIFTS, 1)
        put_gram(a, a_lo, to_bands(below[0].T), to_bands(below[0]), b_lo)
        put_gram(b, a_hi, to_bands(below[1].T), to_bands(below[1]), b_hi)
    reset_turns()
    turn_pairs(gram, turn, pairs)
    put_turns(2)

    for g in range(groups):
        for side, part in ((0, lo), (1, hi)):
            last = turn_ref.at[g, 2 + side]
            top = dot(turn_ref[g, 0, :, part], last[lo, :])
            bottom = dot(turn_ref[g, 1, :, part], last[hi, :])
            rows = [top[lo], top[hi], bottom[lo], bottom[hi]]
            for member, cols in ((side, lo), (2 + side, hi)):
                for i in range(4):
                    coef_ref[4 * g + member, i * w : (i + 1) * w, :] = rows[member ^ i][:, cols]


def on_device(anomalies, pairing):
    count, split = lax.axis_size("cols"), lax.axis_size("rows")
    rows, w = anomalies.shape
    slab = rows // count
    unit = slab // UNITS
    groups = count // 4
    f32 = jnp.float32
    block = 8 * split * count
    total = -(-band_place(groups, 0)[0] // block) * block
    piece = total // (split * count)
    extra = sum(EXTRAS) * unit
    segments = len(PARTS) + len(EXTRAS)
    dma = pltpu.SemaphoreType.DMA
    scratch = {
        "acc": pltpu.VMEM((groups, 3, 2 * w, 2 * w), f32),
        "bands": pltpu.VMEM((total, w), f32),
        "landed": pltpu.VMEM((split, count, piece, w), f32),
        "part": pltpu.VMEM((count, piece, w), f32),
        "slots": pltpu.VMEM((count, piece, w), f32),
        "summed": pltpu.VMEM((total, w), f32),
        "turn_of": pltpu.VMEM((groups, 4, 2 * w, 2 * w), f32),
        "gram": pltpu.VMEM((2, 2 * BAND, 4 * groups, w), f32),
        "turn": pltpu.VMEM((2, 2 * BAND, 4 * groups, w), f32),
        "coef": pltpu.VMEM((4 * groups, 4 * w, w), f32),
        "piece": pltpu.VMEM((count - 1, slab + extra, w), f32),
        "give": dma((len(PARTS), count - 1)),
        "give_s": dma((len(EXTRAS), 4)),
        "get": dma((segments, count)),
        "own": dma((segments,)),
        "rs_s": dma((split, count)),
        "rs_r": dma((split, count)),
        "ag_s": dma((split, count)),
        "ag_r": dma((split, count)),
        "sum_s": dma((2, count)),
        "sum_r": dma((2, count)),
        "back_s": dma((count, segments)),
        "back_r": dma((count, segments)),
    }
    for i, size in enumerate(PARTS):
        scratch["near%d" % i] = pltpu.VMEM((count, size * unit, w), f32)
    for i, size in enumerate(EXTRAS):
        scratch["far%d" % i] = pltpu.VMEM((count, size * unit, w), f32)
    out = pl.pallas_call(
        partial(fused_kernel, count, split, unit, tuple(scratch)),
        out_shape=pltpu.VMEM((count, slab, w), f32),
        in_specs=[
            pl.BlockSpec(memory_space=pltpu.SMEM),
            pl.BlockSpec(memory_space=pl.ANY),
        ],
        out_specs=pl.BlockSpec(memory_space=pltpu.VMEM),
        scratch_shapes=list(scratch.values()),
        compiler_params=pltpu.CompilerParams(collective_id=1, has_side_effects=True),
    )(pairing, anomalies.reshape(count, slab, w))
    return out.reshape(rows, w)


def solution(mesh):
    placed = (P("rows", "cols"), P())
    return jax.shard_map(
        on_device, mesh=mesh, in_specs=placed, out_specs=P("rows", "cols"), check_vma=False
    )
```

```python
from functools import partial

import jax
import jax.numpy as jnp
from jax import lax
from jax.experimental import pallas as pl
from jax.experimental.pallas import tpu as pltpu
from jax.sharding import PartitionSpec as P

SHIFTS = 8
TIE_GUARD = 1e-06
BAND = 2 * SHIFTS
PAIRS = 10
MESH = pl.DeviceIdType.MESH
HIGHEST = lax.Precision.HIGHEST
UNITS = 8
PARTS = (3, 3, 1, 1)
EXTRAS = (1, 1, 6)
POINTS = (0, 2, 3)


def dot(left, right):
    return jnp.dot(left, right, precision=HIGHEST, preferred_element_type=jnp.float32)


def dot_t(left, right):
    return lax.dot_general(
        left,
        right,
        (((0,), (0,)), ((), ())),
        precision=HIGHEST,
        preferred_element_type=jnp.float32,
    )


def halves(value):
    high = value.astype(jnp.bfloat16)
    return high, (value - high.astype(jnp.float32)).astype(jnp.bfloat16)


def quad_blocks(pairing, count, g):
    m0 = pairing[0, 0]
    m1 = pairing[1, 0]
    lower_mask = jnp.minimum(m0, m1)
    low_bits = jnp.int32(0)
    for bit in range(1, count.bit_length() - 1):
        low_bits = jnp.where(lower_mask >= (1 << bit), (1 << bit) - 1, low_bits)
    rest = g & low_bits
    q0 = rest + 2 * (g - rest)
    return q0, q0 ^ m0, q0 ^ m1, q0 ^ (count - 1)


def lane_bit(shape, bit):
    return (lax.broadcasted_iota(jnp.int32, shape, 1) & (1 << bit)) != 0


def to_bands(block):
    w = block.shape[0]
    for bit in range(w.bit_length() - 1):
        block = jnp.where(
            lane_bit(block.shape, bit), pltpu.roll(block, w - (1 << bit), 0), block
        )
    return jnp.concatenate([block[w - BAND :], block[:BAND]], axis=0)


def from_bands(bands):
    w = bands.shape[1]
    block = jnp.concatenate(
        [bands[BAND:], jnp.zeros((w - 2 * BAND, w), jnp.float32), bands[:BAND]], axis=0
    )
    for bit in range(w.bit_length() - 1):
        block = jnp.where(lane_bit(block.shape, bit), pltpu.roll(block, 1 << bit, 0), block)
    return block


def turn_pairs(gram, turn, pairs):
    _, depth, sides, w = gram.shape

    def lane(value):
        return pltpu.roll(value.reshape(depth * sides, w), w - 1, 1).reshape(depth, sides, w)

    def later(value):
        return jnp.concatenate([value[-1:], value[:-1]], axis=0)

    def sooner(value):
        return jnp.concatenate([value[1:], value[:1]], axis=0)

    def swap(value):
        return jnp.concatenate([value[:, pairs:], value[:, :pairs]], axis=1)

    def ahead(value):
        return jnp.stack([pltpu.roll(value, (BAND - r) % w, 1) if r != BAND else value for r in range(depth)])

    lower = lax.broadcasted_iota(jnp.int32, (depth, sides, w), 1) >= pairs

    @pl.loop(0, SHIFTS)
    def _(step):
        g_l, g_r = gram[0], gram[1]
        a, e, g = gram[0, BAND, :pairs], gram[1, BAND, pairs:], gram[1, BAND, :pairs]
        gap = e - a
        sign = jnp.where(gap >= 0.0, 1.0, -1.0)
        denom = jnp.abs(gap) + jnp.sqrt(gap * gap + 4.0 * g * g) + TIE_GUARD * (a + e)
        tangent = 2.0 * g * sign / denom
        cosine = 1.0 / jnp.sqrt(1.0 + tangent * tangent)
        sine = cosine * tangent
        c_2 = jnp.concatenate([cosine, cosine], axis=0)
        s_2 = jnp.concatenate([sine, sine], axis=0)
        c_d = ahead(c_2)
        s_d = ahead(jnp.concatenate([-sine, sine], axis=0))
        t_l = g_l * c_2 - g_r * s_2
        t_r = g_l * s_2 + g_r * c_2
        t_l = c_d * t_l + s_d * swap(t_l)
        t_r = lane(c_d * t_r + s_d * swap(t_r))
        gram[0] = jnp.where(lower, sooner(t_l), t_l)
        gram[1] = jnp.where(lower, t_r, later(t_r))
        v_l, v_r = turn[0], turn[1]
        turn[0] = v_l * c_2 - v_r * s_2
        turn[1] = later(lane(v_l * s_2 + v_r * c_2))


def spans(sizes, unit):
    out, at = [], 0
    for size in sizes:
        out.append((at * unit, (at + size) * unit))
        at += size
    return out


def fused_kernel(count, split, unit, names, pairing, x_ref, out_ref, *refs):
    ref = dict(zip(names, refs))
    near = [ref["near%d" % i] for i in range(len(PARTS))]
    far = [ref["far%d" % i] for i in range(len(EXTRAS))]
    near_at, far_at = spans(PARTS, unit), spans(EXTRAS, unit)
    slab, kept = UNITS * unit, sum(EXTRAS) * unit
    half, groups = count // 2, count // 4
    w = x_ref.shape[2]
    lo, hi = slice(0, w), slice(w, 2 * w)
    me, r = lax.axis_index("cols"), lax.axis_index("rows")
    side, pos = me // half, me % half
    across = [(1 - side) * half + (pos + j) % half for j in range(half)]
    beside = [side * half + (pos + j) % half for j in range(1, half)]
    others = across + beside
    masks = (pairing[0, 0], pairing[1, 0], count - 1)

    def at_end(d):
        return (d < 2) | (d >= count - 2)

    def mirror(d):
        return count - 1 - d

    barrier = pltpu.get_barrier_semaphore()
    for dest in others:
        pl.semaphore_signal(barrier, inc=1, device_id={"cols": dest}, device_id_type=MESH)
    for d in range(1, split):
        pl.semaphore_signal(
            barrier, inc=1, device_id={"rows": (r + d) % split}, device_id_type=MESH
        )
    pl.semaphore_wait(barrier, count + split - 2)

    def remote(src, dst, send, recv, axis, peer):
        return pltpu.make_async_remote_copy(
            src_ref=src,
            dst_ref=dst,
            send_sem=send,
            recv_sem=recv,
            device_id={axis: peer},
            device_id_type=MESH,
        )

    sent = []

    def send(*args, when=None):
        copy = remote(*args)
        sent.append((copy, when))
        if when is None:
            copy.start()
        else:
            pl.when(when)(copy.start)

    def keep(number, land, at, owner):
        rows = pl.ds(at[0], at[1] - at[0])
        return pltpu.make_async_copy(x_ref.at[owner, rows], land.at[me], ref["own"].at[number])

    def give_near(i):
        rows = pl.ds(near_at[i][0], near_at[i][1] - near_at[i][0])
        for n, dest in enumerate(others):
            send(x_ref.at[dest, rows], near[i].at[me], ref["give"].at[i, n], ref["get"].at[i, me], "cols", dest)

    def give_far(i, crossing):
        rows = pl.ds(far_at[i][0], far_at[i][1] - far_at[i][0])
        n = len(PARTS) + i
        base = (1 - side if crossing else side) * (count - 2)
        for e in range(2):
            dest = base + (me + e) % 2
            k = e if crossing else 2 + e
            when = None if crossing else dest != me
            send(x_ref.at[mirror(dest), rows], far[i].at[me], ref["give_s"].at[i, k], ref["get"].at[n, me], "cols", dest, when=when)

    def advance(point):
        for i, when in enumerate(POINTS):
            if when == point:
                give_far(i, True)

    def take(number, land):
        for source in others:
            remote(
                land.at[source], land.at[source], ref["give"].at[0, 0], ref["get"].at[number, source], "cols", source
            ).wait_recv()

    near_keep = [keep(i, near[i], at, me) for i, at in enumerate(near_at)]
    far_keep = [keep(len(PARTS) + i, far[i], at, mirror(me)) for i, at in enumerate(far_at)]
    for copy in near_keep:
        copy.start()
    for copy in far_keep:
        pl.when(at_end(me))(copy.start)
    for i in range(len(PARTS)):
        give_near(i)

    for e in range(len(EXTRAS)):
        give_far(e, False)

    acc, bands = ref["acc"], ref["bands"]
    for i, land in enumerate(near):
        near_keep[i].wait()
        take(i, land)
        if i == len(near) - 1:
            advance(0)
        for g in range(groups):
            x = [land[q] for q in quad_blocks(pairing, count, g)]
            a = jnp.concatenate(x[:2], axis=1)
            b = jnp.concatenate(x[2:], axis=1)
            for k, block in enumerate((dot_t(a, a), dot_t(b, b), dot_t(b, a))):
                acc[g, k] = block if i == 0 else acc[g, k] + block
    places = [(0, lo, lo), (0, hi, lo), (0, hi, hi), (1, lo, lo), (1, hi, lo), (1, hi, hi)]
    places += [(2, lo, lo), (2, lo, hi), (2, hi, lo), (2, hi, hi)]
    for g in range(groups):
        for i, (k, rows, cols) in enumerate(places):
            first, size = band_place(g, i)
            bands[first : first + size] = to_bands(acc[g, k, rows, cols])[2 * BAND - size :]

    landed, slots, part, summed = (ref[n] for n in ("landed", "slots", "part", "summed"))
    piece = slots.shape[1]

    def at(row, col):
        return pl.ds(pl.multiple_of((row * count + col) * piece, piece), piece)

    for k, c in enumerate(others + [me]):
        for d in range(1, split):
            peer = (r + d) % split
            send(bands.at[at(peer, c)], landed.at[d, k], ref["rs_s"].at[d, k], ref["rs_r"].at[d, k], "rows", peer)
    advance(1)
    for k, c in enumerate(others + [me]):
        total = bands[at(r, c)]
        for d in range(1, split):
            peer = (r + split - d) % split
            remote(landed.at[d, k], landed.at[d, k], ref["rs_s"].at[d, k], ref["rs_r"].at[d, k], "rows", peer).wait_recv()
            total = total + landed[d, k]
        part[k] = total
        if k < len(others):
            send(part.at[k], slots.at[me], ref["sum_s"].at[0, k], ref["sum_r"].at[0, me], "cols", c)
    advance(2)
    for c in others:
        remote(slots.at[c], slots.at[c], ref["sum_s"].at[0, 0], ref["sum_r"].at[0, c], "cols", c).wait_recv()
        total = total + slots[c]
    summed[at(r, me)] = total
    mine = summed.at[at(r, me)]

    def spread(source, k):
        for d in range(1, split):
            peer = (r + d) % split
            block = summed.at[at(r, source)]
            send(block, block, ref["ag_s"].at[d, k], ref["ag_r"].at[r, k], "rows", peer)

    for k, c in enumerate(others):
        send(mine, mine, ref["sum_s"].at[1, k], ref["sum_r"].at[1, me], "cols", c)
    spread(me, len(others))
    advance(3)
    for k, c in reversed(list(enumerate(others))):
        block = summed.at[at(r, c)]
        remote(block, block, ref["sum_s"].at[1, k], ref["sum_r"].at[1, c], "cols", c).wait_recv()
        spread(c, k)
    advance(4)
    for d in range(1, split):
        row = (r + d) % split
        for k, c in enumerate(others + [me]):
            block = summed.at[at(row, c)]
            remote(block, block, ref["ag_s"].at[d, k], ref["ag_r"].at[row, k], "rows", row).wait_recv()

    rotate(groups, summed, ref["coef"], ref["turn_of"], ref["gram"], ref["turn"])

    def slot(dest):
        found = jnp.int32(0)
        for g in range(groups):
            for i, q in enumerate(quad_blocks(pairing, count, g)):
                found = jnp.where(q == dest, 4 * g + i, found)
        return found

    def make(dest, coef, buffer):
        blocks = [buffer[dest]] + [buffer[dest ^ mask] for mask in masks]
        high, low = halves(jnp.concatenate(blocks, axis=1))
        product = partial(jnp.dot, preferred_element_type=jnp.float32)
        return product(high, coef[0]) + (product(high, coef[1]) + product(low, coef[0]))

    def place(owner, at):
        return out_ref.at[owner, pl.ds(at[0], at[1] - at[0])]

    end = at_end(me)
    inner = jnp.logical_not(end)
    jobs = [(i, near[i], at, False) for i, at in enumerate(near_at)]
    jobs += [(len(PARTS) + i, far[i], at, True) for i, at in enumerate(far_at)]

    def when_of(job, crossing, whose):
        _, _, at, is_far = job
        if is_far:
            return False if crossing else at_end(whose)
        if crossing and at[0] < kept:
            return jnp.logical_not(at_end(whose))
        return None

    def emit(n, dest, job):
        number, buffer, at, is_far = job
        when = when_of(job, n < half, me)
        if when is False:
            return
        base = slab if is_far else 0
        src = ref["piece"].at[n, pl.ds(base + at[0], at[1] - at[0])]

        def fill():
            src[...] = make(dest, halves(ref["coef"][slot(dest)]), buffer)

        if when is None:
            fill()
        else:
            pl.when(when)(fill)
        dst = place(mirror(me) if is_far else me, at)
        send(src, dst, ref["back_s"].at[n, number], ref["back_r"].at[me, number], "cols", dest, when=when)

    for job in jobs:
        i = job[0] - len(PARTS)
        if i >= 0:
            pl.when(end)(partial(take, job[0], job[1]))
            pl.when(end)(far_keep[i].wait)
        for n, dest in enumerate(others):
            emit(n, dest, job)
    for number, buffer, at, is_far in jobs:

        def fill(buffer=buffer, at=at, is_far=is_far):
            place(mirror(me) if is_far else me, at)[...] = make(me, halves(ref["coef"][slot(me)]), buffer)

        if is_far:
            pl.when(end)(fill)
        else:
            fill()
    for n, source in enumerate(others):
        for job in jobs:
            when = when_of(job, n < half, source)
            if when is False:
                continue
            dst = place(mirror(source) if job[3] else source, job[2])
            copy = remote(dst, dst, ref["back_s"].at[n, job[0]], ref["back_r"].at[source, job[0]], "cols", source)
            if when is None:
                copy.wait_recv()
            else:
                pl.when(when)(copy.wait_recv)
    for copy, when in sent:
        if when is None:
            copy.wait_send()
        else:
            pl.when(when)(copy.wait_send)


def band_place(g, i):
    sizes = [BAND, 2 * BAND, BAND, BAND, 2 * BAND, BAND] + [2 * BAND] * 4
    return g * sum(sizes) + sum(sizes[:i]), sizes[i]


def rotate(groups, band_ref, coef_ref, turn_ref, gram, turn):
    w = band_ref.shape[1]
    pairs = 2 * groups
    lo, hi = slice(0, w), slice(w, 2 * w)

    def bands(g, i):
        start, size = band_place(g, i)
        return band_ref[start : start + size, :]

    def reset_turns():
        shape = turn.shape
        one = lax.broadcasted_iota(jnp.int32, shape, 1) == BAND
        lower = lax.broadcasted_iota(jnp.int32, shape, 2) >= pairs
        right = lax.broadcasted_iota(jnp.int32, shape, 0) == 1
        turn[...] = jnp.where(one & (lower == right), 1.0, 0.0)

    def put_turns(slot):
        for g in range(groups):
            for p in range(2):
                at = 2 * g + p
                for row, side in ((lo, at), (hi, pairs + at)):
                    turn_ref[g, slot + p, row, lo] = from_bands(turn[0, :, side, :])
                    moved = from_bands(turn[1, :, side, :])
                    turn_ref[g, slot + p, row, hi] = pltpu.roll(moved, SHIFTS, 1)

    def put_gram(at, ll, rl, rr):
        gram[0, :, at, :] = ll
        gram[0, :, pairs + at, :] = rl
        gram[1, :, pairs + at, :] = rr

    def put_above():
        gram[1, 0, :pairs, :] = jnp.zeros((pairs, w), jnp.float32)
        for d in range(1 - BAND, BAND):
            gram[1, BAND + d, :pairs, :] = pltpu.roll(gram[0, BAND - d, pairs:, :], -d % w, 1)

    for g in range(groups):
        for p in range(2):
            at = 2 * g + p
            below = bands(g, 3 * p + 1)
            gram[0, BAND:, at, :] = bands(g, 3 * p)
            gram[0, :, pairs + at, :] = below
            gram[1, BAND:, pairs + at, :] = bands(g, 3 * p + 2)
    for k, sides in ((0, slice(0, pairs)), (1, slice(pairs, 2 * pairs))):
        gram[k, 0, sides, :] = jnp.zeros((pairs, w), jnp.float32)
        for d in range(1, BAND):
            gram[k, BAND - d, sides, :] = pltpu.roll(gram[k, BAND + d, sides, :], d, 1)
    put_above()
    reset_turns()
    turn_pairs(gram, turn, pairs)
    put_turns(0)

    for g in range(groups):
        blocks = [from_bands(bands(g, 6 + i)) for i in range(4)]
        cross = jnp.concatenate(
            [
                jnp.concatenate([blocks[0], blocks[1]], axis=1),
                jnp.concatenate([blocks[2], blocks[3]], axis=1),
            ],
            axis=0,
        )
        half = dot(cross, turn_ref[g, 0])
        below = [
            dot_t(turn_ref[g, 1, :, lo], half[:, lo]),
            dot_t(turn_ref[g, 1, :, hi], half[:, hi]),
        ]
        a, b = 2 * g, 2 * g + 1
        a_lo, b_lo = gram[0, :, a, :], gram[0, :, b, :]
        a_hi = pltpu.roll(gram[1, :, pairs + a, :], SHIFTS, 1)
        b_hi = pltpu.roll(gram[1, :, pairs + b, :], SHIFTS, 1)
        put_gram(a, a_lo, to_bands(below[0]), b_lo)
        put_gram(b, a_hi, to_bands(below[1]), b_hi)
    put_above()
    reset_turns()
    turn_pairs(gram, turn, pairs)
    put_turns(2)

    for g in range(groups):
        for side, part in ((0, lo), (1, hi)):
            last = turn_ref.at[g, 2 + side]
            top = dot(turn_ref[g, 0, :, part], last[lo, :])
            bottom = dot(turn_ref[g, 1, :, part], last[hi, :])
            rows = [top[lo], top[hi], bottom[lo], bottom[hi]]
            for member, cols in ((side, lo), (2 + side, hi)):
                for i in range(4):
                    coef_ref[4 * g + member, i * w : (i + 1) * w, :] = rows[member ^ i][:, cols]


def on_device(anomalies, pairing):
    count, split = lax.axis_size("cols"), lax.axis_size("rows")
    rows, w = anomalies.shape
    slab = rows // count
    unit = slab // UNITS
    groups = count // 4
    f32 = jnp.float32
    block = 8 * split * count
    total = -(-band_place(groups, 0)[0] // block) * block
    piece = total // (split * count)
    extra = sum(EXTRAS) * unit
    segments = len(PARTS) + len(EXTRAS)
    dma = pltpu.SemaphoreType.DMA
    scratch = {
        "acc": pltpu.VMEM((groups, 3, 2 * w, 2 * w), f32),
        "bands": pltpu.VMEM((total, w), f32),
        "landed": pltpu.VMEM((split, count, piece, w), f32),
        "part": pltpu.VMEM((count, piece, w), f32),
        "slots": pltpu.VMEM((count, piece, w), f32),
        "summed": pltpu.VMEM((total, w), f32),
        "turn_of": pltpu.VMEM((groups, 4, 2 * w, 2 * w), f32),
        "gram": pltpu.VMEM((2, 2 * BAND, 4 * groups, w), f32),
        "turn": pltpu.VMEM((2, 2 * BAND, 4 * groups, w), f32),
        "coef": pltpu.VMEM((4 * groups, 4 * w, w), f32),
        "piece": pltpu.VMEM((count - 1, slab + extra, w), f32),
        "give": dma((len(PARTS), count - 1)),
        "give_s": dma((len(EXTRAS), 4)),
        "get": dma((segments, count)),
        "own": dma((segments,)),
        "rs_s": dma((split, count)),
        "rs_r": dma((split, count)),
        "ag_s": dma((split, count)),
        "ag_r": dma((split, count)),
        "sum_s": dma((2, count)),
        "sum_r": dma((2, count)),
        "back_s": dma((count, segments)),
        "back_r": dma((count, segments)),
    }
    for i, size in enumerate(PARTS):
        scratch["near%d" % i] = pltpu.VMEM((count, size * unit, w), f32)
    for i, size in enumerate(EXTRAS):
        scratch["far%d" % i] = pltpu.VMEM((count, size * unit, w), f32)
    out = pl.pallas_call(
        partial(fused_kernel, count, split, unit, tuple(scratch)),
        out_shape=pltpu.VMEM((count, slab, w), f32),
        in_specs=[
            pl.BlockSpec(memory_space=pltpu.SMEM),
            pl.BlockSpec(memory_space=pl.ANY),
        ],
        out_specs=pl.BlockSpec(memory_space=pltpu.VMEM),
        scratch_shapes=list(scratch.values()),
        compiler_params=pltpu.CompilerParams(collective_id=1, has_side_effects=True),
    )(pairing, anomalies.reshape(count, slab, w))
    return out.reshape(rows, w)


def solution(mesh):
    placed = (P("rows", "cols"), P())
    return jax.shard_map(
        on_device, mesh=mesh, in_specs=placed, out_specs=P("rows", "cols"), check_vma=False
    )
```
